768 devices in a mesh: dom: 24 (over y_hi, z), sub: 32 (over x, y_lo, core).
Axes of the slice: x: 4, y: 8 (y_hi: 2, y_lo: 4; y = y_hi * 4 + y_lo), z: 12, core: 2. Of those that a mesh axis runs over, the one named last changes fastest.
Arguments:
- coefficients: float32 [9, 56, 98304], P(None, None, ('dom', 'sub')), may hold values from -6 to 6
- stiffness: float32 [3, 56, 56], replicated, may hold values from -0.75 to 0.75
- jacobians: float32 [3, 9, 9, 98304], P(None, None, None, ('dom', 'sub')), may hold values from -1.25 to 1.25
- face_proj: float32 [4, 21, 56], replicated, may hold values from -0.75 to 0.75
- neigh_proj: float32 [12, 21, 56], replicated, may hold values from -0.75 to 0.75
- lifting: float32 [4, 56, 21], replicated, may hold values from -1.25 to 1.25
- flux_local: float32 [4, 9, 9, 98304], P(None, None, None, ('dom', 'sub')), may hold values from -2 to 2
- flux_neigh: float32 [4, 9, 9, 98304], P(None, None, None, ('dom', 'sub')), may hold values from -2 to 2
- clusters: int32 [98304], P(('dom', 'sub')), may hold values from 0 to 2
- face_slots: int32 [4, 98304], P(None, ('dom', 'sub')), may hold values from 0 to 192, as said below
- orientation: int32 [4, 98304], P(None, ('dom', 'sub')), may hold values from 0 to 11
- send_list: int32 [4, 12288], P(None, ('dom', 'sub')), may hold values from 0 to 127, as said below
Outputs:
- increment: float32 [9, 56, 98304], P(None, None, ('dom', 'sub'))
The draws below stay inside these ranges and needn't reach their ends.
Inputs may be any that keep to these rules, and one draw needn't show every extreme that they name: `face_slots`: A face refers to another local element (entry below 128, never the element itself), to a received element, or to the last entry (no neighbour). Every received entry of a neighbour that exists is referred to by exactly one face of the partition; entries of neighbours that do not exist are never referred to. `send_list`: the 16 entries of one row of one partition are distinct local element numbers.
All inputs are finite; a program needn't handle non-finite values.
Results may differ from the reference program's by a relative error of at most 0.0003.
Values sent between devices are 32-bit elements; how exact they have to be, the bound alone decides.
A program may use at most 192 MiB of HBM per device.

```python
import math
import jax
import jax.numpy as jnp
from jax import lax

FIELDS = 9
BASIS = 56
FACE_BASIS = 21
ORDER = 6
ORIENTS = 12
SUBSTEPS = 4
E_DEV = 128
BSEND = 16
GROUPS = 24
SUBS = 32
PARTITIONS = 768
ELEMS = 98304


def draw_face_slots(key, part):

    def draw_device(device):
        device_key = jax.random.fold_in(key, device)
        key_local, key_rim, key_cross = jax.random.split(device_key, 3)
        positions = jnp.arange(E_DEV, dtype=jnp.int32)[None, :]
        local_slot = (positions + 1 + jax.random.randint(key_local, (4, E_DEV), 0, E_DEV - 1)) % E_DEV
        rim_mask = jax.random.randint(key_rim, (4, E_DEV), 0, 16) == 0
        slots_flat = jnp.where(rim_mask, E_DEV + 4 * BSEND, local_slot).reshape(-1).astype(jnp.int32)
        chosen = jax.random.permutation(key_cross, 4 * E_DEV)[:4 * BSEND]
        sub_pos = device % SUBS
        group_pos = device // SUBS
        direction = jnp.arange(4 * BSEND, dtype=jnp.int32) // BSEND
        has_peer = jnp.where(direction == 0, sub_pos > 0, jnp.where(direction == 1, sub_pos < SUBS - 1, jnp.where(direction == 2, group_pos > 0, group_pos < GROUPS - 1)))
        cross_slot = jnp.where(has_peer, E_DEV + jnp.arange(4 * BSEND, dtype=jnp.int32), E_DEV + 4 * BSEND).astype(jnp.int32)
        slots_flat = slots_flat.at[chosen].set(cross_slot)
        return slots_flat.reshape(4, E_DEV)
    per_device = jax.vmap(draw_device)(jnp.arange(PARTITIONS, dtype=jnp.int32))
    return jnp.moveaxis(per_device, 0, 1).reshape(4, PARTITIONS * E_DEV).astype(jnp.int32)


def draw_send_list(key, part):

    def draw_device(device):
        device_key = jax.random.fold_in(key, device + 7919)
        row_keys = jax.random.split(device_key, 4)
        rows_list = [jax.random.permutation(row_keys[index], E_DEV)[:BSEND] for index in range(4)]
        return jnp.stack(rows_list).astype(jnp.int32)
    per_device = jax.vmap(draw_device)(jnp.arange(PARTITIONS, dtype=jnp.int32))
    return jnp.moveaxis(per_device, 0, 1).reshape(4, PARTITIONS * BSEND).astype(jnp.int32)


def set_ends(values, stream_key, low, high):
    spot = [jax.random.randint(jax.random.fold_in(stream_key, axis), (), 0, length) for axis, length in enumerate(values.shape)]
    widest = values.shape.index(max(values.shape))
    beside = spot[:widest] + [(spot[widest] + 1) % values.shape[widest]] + spot[widest + 1:]
    return values.at[tuple(spot)].set(low).at[tuple(beside)].set(high)


def block_levels(rng, extent, cuts, smallest, largest):
    level, own = 1.0, jax.random.fold_in(rng, 6)
    for axis_at, blocks in cuts:
        draws = jnp.exp(jax.random.uniform(jax.random.fold_in(own, axis_at), (blocks,), jnp.float32, smallest / len(cuts), largest / len(cuts)))
        level = level * jnp.repeat(draws, extent[axis_at] // blocks).reshape([-1 if axis == axis_at else 1 for axis in range(len(extent))])
    return level


def centred(rng, shape, width, reach, cuts=(), kind=jnp.bfloat16):
    drawn = jax.random.normal(rng, shape, jnp.float32) * width
    if len(cuts) > 0:
        drawn = block_levels(rng, shape, cuts, -0.22, 0.18) * drawn
    return jnp.clip(drawn, min=-reach, max=reach).astype(kind)


def setup_inputs(seed: int = 0) -> dict:
    key_of = jax.random.split(jax.random.key(seed), 13)
    return {
        "coefficients": centred(key_of[0], (FIELDS, BASIS, ELEMS), 1.0, 6.0, ((2, 768),), jnp.float32),
        "stiffness": centred(key_of[1], (3, BASIS, BASIS), BASIS ** -0.5, 0.75, (), jnp.float32),
        "jacobians": centred(key_of[2], (3, FIELDS, FIELDS, ELEMS), (3 * FIELDS) ** -0.5, 1.25, ((3, 768),), jnp.float32),
        "face_proj": centred(key_of[3], (4, FACE_BASIS, BASIS), BASIS ** -0.5, 0.75, (), jnp.float32),
        "neigh_proj": centred(key_of[4], (ORIENTS, FACE_BASIS, BASIS), BASIS ** -0.5, 0.75, (), jnp.float32),
        "lifting": centred(key_of[5], (4, BASIS, FACE_BASIS), FACE_BASIS ** -0.5, 1.25, (), jnp.float32),
        "flux_local": centred(key_of[6], (4, FIELDS, FIELDS, ELEMS), FIELDS ** -0.5, 2.0, ((3, 768),), jnp.float32),
        "flux_neigh": centred(key_of[7], (4, FIELDS, FIELDS, ELEMS), FIELDS ** -0.5, 2.0, ((3, 768),), jnp.float32),
        "clusters": set_ends(jax.random.randint(key_of[8], (ELEMS,), 0, 3), jax.random.fold_in(key_of[8], 1), 0, 2).astype(jnp.int32),
        "face_slots": draw_face_slots(jax.random.fold_in(key_of[12], 71), 0),
        "orientation": set_ends(jax.random.randint(key_of[10], (4, ELEMS), 0, ORIENTS), jax.random.fold_in(key_of[10], 1), 0, ORIENTS - 1).astype(jnp.int32),
        "send_list": draw_send_list(jax.random.fold_in(key_of[12], 71), 0),
    }


HIGHEST = lax.Precision.HIGHEST
STEP_LENGTH = 0.5


def derivatives(values, jacobians, stiffness):
    result = [values]
    current = values
    for degree in range(ORDER - 1):
        spatial = jnp.einsum("dab,qbe->dqae", stiffness, current, precision=HIGHEST)
        current = -jnp.einsum("dpqe,dqae->pae", jacobians, spatial, precision=HIGHEST)
        result.append(current)
    return result


def integrate(series, lower_time, upper_time):
    summed = jnp.zeros_like(series[0])
    for degree in range(ORDER):
        weight = (upper_time ** (degree + 1) - lower_time ** (degree + 1)) / math.factorial(degree + 1)
        summed = summed + series[degree] * weight
    return summed


def windows(clusters, substep):
    length = jnp.where(clusters == 0, 1, jnp.where(clusters == 1, 2, 4)).astype(jnp.int32)
    phase_index = substep % length
    lower_time = phase_index.astype(jnp.float32) * STEP_LENGTH
    finished = (substep + 1) % length == 0
    return lower_time, lower_time + STEP_LENGTH, finished


def contribution(own_part, neighbours, jacobians, flux_local, flux_neigh, orientation, stiffness, face_proj, neigh_proj, lifting):
    volume = jnp.einsum("dba,qbe->dqae", stiffness, own_part, precision=HIGHEST)
    volume = jnp.einsum("dpqe,dqae->pae", jacobians, volume, precision=HIGHEST)
    traces = jnp.einsum("fcb,qbe->fqce", face_proj, own_part, precision=HIGHEST)
    local_flux = jnp.einsum("fpqe,fqce->fpce", flux_local, traces, precision=HIGHEST)
    local_term = jnp.einsum("fac,fpce->pae", lifting, local_flux, precision=HIGHEST)
    matrices = neigh_proj[orientation]
    outer_trace = jnp.einsum("fecb,qbfe->fqce", matrices, neighbours, precision=HIGHEST)
    neigh_flux = jnp.einsum("fpqe,fqce->fpce", flux_neigh, outer_trace, precision=HIGHEST)
    neigh_term = jnp.einsum("fac,fpce->pae", lifting, neigh_flux, precision=HIGHEST)
    return volume - local_term - neigh_term


def neighbour_table(face_slots, send_list):
    element = jnp.arange(ELEMS, dtype=jnp.int32)[None, :]
    device = element // E_DEV
    sub_pos = device % SUBS
    group_pos = device // SUBS
    is_local = face_slots < E_DEV
    is_recv = (face_slots >= E_DEV) & (face_slots < E_DEV + 4 * BSEND)
    relative = jnp.clip(face_slots - E_DEV, 0, 4 * BSEND - 1)
    direction = relative // BSEND
    position = relative % BSEND
    offsets = jnp.array([-1, 1, -SUBS, SUBS], dtype=jnp.int32)[direction]
    source_row = jnp.array([1, 0, 3, 2], dtype=jnp.int32)[direction]
    has_peer = jnp.where(direction == 0, sub_pos > 0, jnp.where(direction == 1, sub_pos < SUBS - 1, jnp.where(direction == 2, group_pos > 0, group_pos < GROUPS - 1)))
    source = jnp.clip(device + offsets, 0, PARTITIONS - 1).astype(jnp.int32)
    sender = send_list[source_row, source * BSEND + position]
    remote = source * E_DEV + sender
    result = jnp.where(is_local, device * E_DEV + face_slots, jnp.where(is_recv & has_peer, remote, ELEMS))
    return result.astype(jnp.int32)


def reference(coefficients, stiffness, jacobians, face_proj, neigh_proj, lifting, flux_local, flux_neigh, clusters, face_slots, orientation, send_list):
    neighbour_ids = neighbour_table(face_slots, send_list)

    def to_blocks(array):
        return jnp.moveaxis(array.reshape(array.shape[:-1] + (PARTITIONS, E_DEV)), -2, 0)

    def from_blocks(array):
        moved = jnp.moveaxis(array, 0, -2)
        return moved.reshape(moved.shape[:-2] + (PARTITIONS * E_DEV,))

    jacobian_blocks = to_blocks(jacobians)
    local_blocks = to_blocks(flux_local)
    neigh_blocks = to_blocks(flux_neigh)
    orient_blocks = to_blocks(orientation)
    id_blocks = to_blocks(neighbour_ids)
    applied = jnp.zeros_like(coefficients)
    pending = jnp.zeros_like(coefficients)
    for substep in range(SUBSTEPS):
        current = coefficients + applied
        lower_time, upper_time, finished = windows(clusters, substep)

        def predict(operands):
            values, jacobian_part, lower_part, upper_part = operands
            return integrate(derivatives(values, jacobian_part, stiffness), lower_part, upper_part)

        own_part = from_blocks(lax.map(predict, (to_blocks(current), jacobian_blocks, to_blocks(lower_time), to_blocks(upper_time))))
        padded = jnp.concatenate([own_part, jnp.zeros((FIELDS, BASIS, 1), own_part.dtype)], axis=2)

        def update(operands):
            own_block, id_block, jacobian_part, local_part, neigh_part, orient_part = operands
            neighbours = padded[:, :, id_block]
            return contribution(own_block, neighbours, jacobian_part, local_part, neigh_part, orient_part, stiffness, face_proj, neigh_proj, lifting)

        change = from_blocks(lax.map(update, (to_blocks(own_part), id_blocks, jacobian_blocks, local_blocks, neigh_blocks, orient_blocks)))
        pending = pending + change
        applied = applied + jnp.where(finished, pending, 0.0)
        pending = jnp.where(finished, 0.0, pending)
    return applied
```

```python
import math

import jax
import jax.numpy as jnp
from jax import lax
from jax.experimental import pallas as pl
from jax.experimental.pallas import tpu as pltpu
from jax.sharding import PartitionSpec as P

Q = 9
B = 56
C = 21
CP = 24
E = 128
R = 16
ORDER = 6
ORIENTS = 12
SUBSTEPS = 4
STEP_LENGTH = 0.5
F32 = jnp.float32
BF16 = jnp.bfloat16
MESH = pl.DeviceIdType.MESH
OPPOSITE = (1, 0, 3, 2)
NT = (((1,), (1,)), ((), ()))
HIGHEST = lax.Precision.HIGHEST


def iota(shape, dim):
    return lax.broadcasted_iota(jnp.int32, shape, dim)


def halves(x):
    hi = x.astype(BF16)
    return hi, (x - hi.astype(F32)).astype(BF16)


def mm(a, b):
    return jnp.dot(a, b, preferred_element_type=F32)


def exact(a, b):
    return jnp.dot(a, b, preferred_element_type=F32, precision=HIGHEST)


def onehot(cond):
    return jnp.where(cond, 1.0, 0.0).astype(BF16)


def kernel(
    coef, stiff, jac, fproj, nproj, lift, floc, fnei, clus, slots, orient, slist,
    out,
    wf, w_d, w_u, w_n, w_l, oh_loc, oh_rem, oh_send, or_rem,
    rhs, sp, own, upd, app, pend, wt, trn, tn, tl_hi, tl_lo, flux, rhs_l, rhs_r, tt,
    send, recv, send_sem, recv_sem,
):
    sub, dom = lax.axis_index("sub"), lax.axis_index("dom")
    subs, doms = lax.axis_size("sub"), lax.axis_size("dom")
    peers = ({"sub": sub - 1}, {"sub": sub + 1}, {"dom": dom - 1}, {"dom": dom + 1})
    has = (sub > 0, sub < subs - 1, dom > 0, dom < doms - 1)
    barrier = pltpu.get_barrier_semaphore()
    for r in range(4):
        @pl.when(has[r])
        def _():
            pl.semaphore_signal(barrier, inc=1, device_id=peers[r], device_id_type=MESH)

        @pl.when(jnp.logical_not(has[r]))
        def _():
            for j in range(SUBSTEPS):
                recv[j, r] = jnp.zeros((R, 512), F32)

    def copy(j, r, slot):
        return pltpu.make_async_remote_copy(
            src_ref=send.at[j, r],
            dst_ref=recv.at[j, slot],
            send_sem=send_sem.at[j, r],
            recv_sem=recv_sem.at[j, slot],
            device_id=peers[r],
            device_id_type=MESH,
        )

    def triple(rows, width, step, x):
        place = jnp.where(
            (iota((x.shape[1], width), 1) % step == iota((x.shape[1], width), 0))
            & (iota((x.shape[1], width), 1) < 3 * step), 1.0, 0.0)
        return exact(x, place)

    def pack(x, step):
        hi = x.astype(BF16).astype(F32)
        return jnp.where(iota(x.shape, 1) < 2 * step, hi, x - hi).astype(BF16)

    for d in range(3):
        wf[d * B:(d + 1) * B, :] = triple(B, 192, 64, stiff[d])
    w_d[...] = pack(wf[0:3 * B, :], 64)

    def prepare_send():
        rows = iota((64, R), 0)
        picked = slist[0:1, :]
        picked = jnp.where(rows // R == 0, slist[0:1, :], jnp.where(
            rows // R == 1, slist[1:2, :], jnp.where(
                rows // R == 2, slist[2:3, :], slist[3:4, :])))
        picked = jnp.where(rows % R == iota((64, R), 1), picked.astype(F32), 0.0)
        column = jnp.sum(picked, axis=1, keepdims=True)
        oh_send[...] = onehot(iota((64, E), 1).astype(F32) == column)

    def prepare_rest():
        eye = jnp.where(iota((B, B), 0) == iota((B, B), 1), 1.0, 0.0)
        for d in range(3):
            turned = lax.dot_general(eye, stiff[d], NT, precision=HIGHEST, preferred_element_type=F32)
            wf[d * B:(d + 1) * B, :] = triple(B, 192, 64, turned)
        zero = jnp.zeros((CP - C, 192), F32)
        for f in range(4):
            wf[3 * B + f * CP:3 * B + (f + 1) * CP, :] = jnp.concatenate(
                [triple(C, 192, 64, fproj[:, f, :]), zero], axis=0)
        w_u[...] = pack(wf[0:3 * B + 4 * CP, :], 64)
        for o in range(ORIENTS):
            wf[o * CP:(o + 1) * CP, :] = jnp.concatenate(
                [triple(C, 192, 64, nproj[o]), zero], axis=0)
        w_n[...] = pack(wf[...], 64)
        total = None
        for f in range(4):
            spot = iota((C, 288), 1)
            place = jnp.where(spot % 96 == iota((C, 288), 0) + f * CP, 1.0, 0.0)
            turned = lax.dot_general(eye, lift[:, f, :], NT, precision=HIGHEST, preferred_element_type=F32)
            part = exact(turned, place)
            total = part if total is None else total + part
        w_l[...] = pack(total, 96)
        for f in range(4):
            cols = slice(f * E, (f + 1) * E)
            row = jnp.broadcast_to(slots[f:f + 1, :], (E, E))
            pair = jnp.broadcast_to(orient[f:f + 1, :], (E, E))
            here = onehot(iota((E, E), 0) == row)
            for o in range(ORIENTS):
                oh_loc[o * E:(o + 1) * E, cols] = here * onehot(pair == o)
            entry = iota((E, E), 0)
            first = onehot(entry + E == row) * onehot(entry < 64)
            second = onehot(entry + 64 == row) * onehot(entry >= 64)
            for k in range(2):
                oh_rem[k * E:(k + 1) * E, f * E:(f + 1) * E] = first
                oh_rem[k * E:(k + 1) * E, 512 + f * E:512 + (f + 1) * E] = second
        total = None
        for f in range(4):
            row = jnp.broadcast_to(orient[f:f + 1, :].astype(F32), (8, E)).astype(BF16)
            both = oh_rem[0:E, f * E:(f + 1) * E] + oh_rem[0:E, 512 + f * E:512 + (f + 1) * E]
            part = lax.dot_general(row, both, NT, preferred_element_type=F32)
            total = part if total is None else total + part
        or_rem[...] = total

    prepare_send()
    app[...] = jnp.zeros((Q, B, E), F32)
    pend[...] = jnp.zeros((Q, B, E), F32)

    def split_store(x, q):
        hi, lo = halves(jnp.concatenate([x, jnp.zeros((64 - B, E), F32)], axis=0))
        cols = pl.ds(q * E if isinstance(q, int) else pl.multiple_of(q * E, E), E)
        rhs[0:64, cols] = hi
        rhs[64:128, cols] = lo
        rhs[128:192, cols] = hi

    def mix(g):
        acc = None
        for q in range(Q):
            for d in range(3):
                term = jac[pl.ds(3 * g, 3), q, d:d + 1, :] * sp[d * B:(d + 1) * B, q * E:(q + 1) * E][None]
                acc = term if acc is None else acc + term
        return acc

    def face_mix(g, f, flow, trace, acc=None):
        for q in range(Q):
            term = flow[pl.ds(3 * g, 3), q, f:f + 1, :] * trace(q)[None]
            acc = term if acc is None else acc + term
        return acc

    def substep(j, carry):
        c = clus[0:1, :]
        length = jnp.where(c == 0, 1, jnp.where(c == 1, 2, 4)).astype(jnp.int32)
        lower = (jnp.bitwise_and(j, length - 1)).astype(F32) * STEP_LENGTH
        upper = lower + STEP_LENGTH
        low_power, up_power = lower, upper
        for k in range(ORDER):
            wt[k:k + 1, :] = (up_power - low_power) * ((-1.0) ** k / math.factorial(k + 1))
            low_power, up_power = low_power * lower, up_power * upper
        for q in range(Q):
            current = coef[q] + app[q]
            own[q] = current * wt[0:1, :]
            split_store(current, q)

        def degree(k, carry):
            sp[0:3 * B, :] = mm(w_d[...], rhs[...])
            weight = wt[pl.ds(k, 1), :]

            def group(g, carry):
                acc = mix(g)
                own[pl.ds(3 * g, 3)] = own[pl.ds(3 * g, 3)] + acc * weight[None]
                for i in range(3):
                    split_store(acc[i], 3 * g + i)
                return carry

            lax.fori_loop(0, 3, group, 0)
            return carry

        lax.fori_loop(1, ORDER, degree, 0)

        flat = jnp.concatenate([own[...].reshape(Q * B, E), jnp.zeros((8, E), F32)], axis=0)
        hi, lo = halves(flat)
        picked = lax.dot_general(oh_send[...], hi, NT, preferred_element_type=F32)
        picked = picked + lax.dot_general(oh_send[...], lo, NT, preferred_element_type=F32)
        for r in range(4):
            send[j, r] = picked[r * R:(r + 1) * R, :]

        @pl.when(j == 0)
        def _():
            pl.semaphore_wait(barrier, sum(jnp.where(h, 1, 0) for h in has))

        for r in (3, 2, 1, 0):
            @pl.when(has[r])
            def _():
                copy(j, r, OPPOSITE[r]).start()

        @pl.when(j == 0)
        def _():
            prepare_rest()

        for q in range(Q):
            split_store(own[q], q)
        sp[...] = mm(w_u[...], rhs[...])

        def local(g, carry):
            upd[pl.ds(3 * g, 3)] = mix(g)
            for f in range(4):
                rows = slice(3 * B + f * CP, 3 * B + (f + 1) * CP)
                flux[pl.ds(3 * g, 3), f * CP:(f + 1) * CP, :] = face_mix(
                    g, f, floc, lambda q: sp[rows, q * E:(q + 1) * E])
            return carry

        lax.fori_loop(0, 3, local, 0)
        tn[...] = mm(w_n[...], rhs[...])

        def turn(o, carry):
            rows = pl.ds(pl.multiple_of(o * CP, CP), CP)
            cols = pl.ds(pl.multiple_of(o * E, E), E)
            hi, lo = halves(jnp.concatenate([tn[rows, q * E:(q + 1) * E] for q in range(Q)], axis=0))
            tl_hi[:, cols] = hi
            tl_lo[:, cols] = lo
            return carry

        lax.fori_loop(0, ORIENTS, turn, 0)

        def near(n, carry):
            cols = pl.ds(pl.multiple_of(n * 256, 256), 256)
            trn[:, cols] = mm(tl_hi[...], oh_loc[:, cols]) + mm(tl_lo[...], oh_loc[:, cols])
            return carry

        lax.fori_loop(0, 2, near, 0)

        for r in range(4):
            @pl.when(has[r])
            def _():
                copy(j, r, r).wait_recv()

        got = recv[j].reshape(64, 512)
        tt[...] = jnp.concatenate([got, got], axis=0).T
        left = iota((B, E), 1) < 64
        for i in range(5):
            first = tt[2 * i * B:(2 * i + 1) * B, :]
            second = tt[(2 * i + 1) * B:(2 * i + 2) * B, :] if i < 4 else first
            x = jnp.where(left, first, second)
            hi, lo = halves(jnp.concatenate([x, jnp.zeros((64 - B, E), F32)], axis=0))
            cols = slice(i * E, (i + 1) * E)
            rhs_r[0:64, cols] = hi
            rhs_r[64:128, cols] = lo
            rhs_r[128:192, cols] = hi
        traces = mm(w_n[...], rhs_r[...])
        pair = jnp.broadcast_to(or_rem[0:1, :], (CP, E))
        parts = []
        for i in range(5):
            cols = slice(i * E, (i + 1) * E)
            chosen = traces[0:CP, cols]
            for o in range(1, ORIENTS):
                chosen = jnp.where(pair == float(o), traces[o * CP:(o + 1) * CP, cols], chosen)
            parts.append(chosen)
        hi, lo = halves(jnp.concatenate(parts, axis=0))
        far = mm(jnp.concatenate([hi, lo], axis=1), oh_rem[...])
        for q in range(Q):
            rows = slice(q * CP, (q + 1) * CP)
            trn[rows, :] = trn[rows, :] + far[
                (q // 2) * CP:(q // 2 + 1) * CP, (q % 2) * 512:(q % 2) * 512 + 512]

        def outer(g, carry):
            parts = []
            for f in range(4):
                parts.append(face_mix(
                    g, f, fnei, lambda q: trn[q * CP:(q + 1) * CP, f * E:(f + 1) * E],
                    flux[pl.ds(3 * g, 3), f * CP:(f + 1) * CP, :]))
            for i in range(3):
                hi, lo = halves(jnp.concatenate([part[i] for part in parts], axis=0))
                cols = pl.ds(pl.multiple_of((3 * g + i) * E, E), E)
                rhs_l[0:96, cols] = hi
                rhs_l[96:192, cols] = lo
                rhs_l[192:288, cols] = hi
            return carry

        lax.fori_loop(0, 3, outer, 0)
        lifted = mm(w_l[...], rhs_l[...])
        finished = jnp.broadcast_to(jnp.where(jnp.bitwise_and(j + 1, length - 1) == 0, 1.0, 0.0), (B, E)) > 0.5
        for p in range(Q):
            total = pend[p] + (upd[p] - lifted[:, p * E:(p + 1) * E])
            app[p] = app[p] + jnp.where(finished, total, 0.0)
            pend[p] = jnp.where(finished, 0.0, total)
        return carry

    lax.fori_loop(0, SUBSTEPS, substep, 0)
    out[...] = app[...]

    def drain(j, carry):
        for r in range(4):
            @pl.when(has[r])
            def _():
                copy(j, r, OPPOSITE[r]).wait_send()
        return carry

    lax.fori_loop(0, SUBSTEPS, drain, 0)


def on_device(coefficients, stiffness, jacobians, face_proj, neigh_proj, lifting, flux_local,
              flux_neigh, clusters, face_slots, orientation, send_list):
    vmem = pl.BlockSpec(memory_space=pltpu.VMEM)
    return pl.pallas_call(
        kernel,
        out_shape=jax.ShapeDtypeStruct((Q, B, E), F32),
        in_specs=[vmem] * 12,
        out_specs=vmem,
        scratch_shapes=[
            pltpu.VMEM((288, 192), F32),
            pltpu.VMEM((168, 192), BF16),
            pltpu.VMEM((264, 192), BF16),
            pltpu.VMEM((288, 192), BF16),
            pltpu.VMEM((B, 288), BF16),
            pltpu.VMEM((ORIENTS * E, 512), BF16),
            pltpu.VMEM((256, 1024), BF16),
            pltpu.VMEM((64, E), BF16),
            pltpu.VMEM((8, E), F32),
            pltpu.VMEM((192, Q * E), BF16),
            pltpu.VMEM((264, Q * E), F32),
            pltpu.VMEM((Q, B, E), F32),
            pltpu.VMEM((Q, B, E), F32),
            pltpu.VMEM((Q, B, E), F32),
            pltpu.VMEM((Q, B, E), F32),
            pltpu.VMEM((8, E), F32),
            pltpu.VMEM((Q * CP, 512), F32),
            pltpu.VMEM((288, Q * E), F32),
            pltpu.VMEM((Q * CP, ORIENTS * E), BF16),
            pltpu.VMEM((Q * CP, ORIENTS * E), BF16),
            pltpu.VMEM((Q, 96, E), F32),
            pltpu.VMEM((288, Q * E), BF16),
            pltpu.VMEM((192, 640), BF16),
            pltpu.VMEM((512, E), F32),
            pltpu.VMEM((SUBSTEPS, 4, R, 512), F32),
            pltpu.VMEM((SUBSTEPS, 4, R, 512), F32),
            pltpu.SemaphoreType.DMA((SUBSTEPS, 4)),
            pltpu.SemaphoreType.DMA((SUBSTEPS, 4)),
        ],
        compiler_params=pltpu.CompilerParams(collective_id=0, has_side_effects=True),
    )(coefficients, stiffness, jacobians.transpose(1, 2, 0, 3), face_proj.transpose(1, 0, 2), neigh_proj,
      lifting.transpose(2, 0, 1), flux_local.transpose(1, 2, 0, 3), flux_neigh.transpose(1, 2, 0, 3),
      clusters.reshape(1, E), face_slots, orientation, send_list)


def solution(mesh):
    placed = (
        P(None, None, ("dom", "sub")),
        P(),
        P(None, None, None, ("dom", "sub")),
        P(),
        P(),
        P(),
        P(None, None, None, ("dom", "sub")),
        P(None, None, None, ("dom", "sub")),
        P(("dom", "sub")),
        P(None, ("dom", "sub")),
        P(None, ("dom", "sub")),
        P(None, ("dom", "sub")),
    )
    return jax.shard_map(
        on_device,
        mesh=mesh,
        in_specs=placed,
        out_specs=P(None, None, ("dom", "sub")),
        check_vma=False,
    )
```

```python
import math

import jax
import jax.numpy as jnp
from jax import lax
from jax.experimental import pallas as pl
from jax.experimental.pallas import tpu as pltpu
from jax.sharding import PartitionSpec as P

Q = 9
B = 56
C = 21
CP = 24
E = 128
R = 16
ORDER = 6
ORIENTS = 12
SUBSTEPS = 4
STEP_LENGTH = 0.5
F32 = jnp.float32
BF16 = jnp.bfloat16
MESH = pl.DeviceIdType.MESH
OPPOSITE = (1, 0, 3, 2)
NT = (((1,), (1,)), ((), ()))


def iota(shape, dim):
    return lax.broadcasted_iota(jnp.int32, shape, dim)


def halves(x):
    hi = x.astype(BF16)
    return hi, (x - hi.astype(F32)).astype(BF16)


def mm(a, b):
    return jnp.dot(a, b, preferred_element_type=F32)


def onehot(cond):
    return jnp.where(cond, 1.0, 0.0).astype(BF16)


def kernel(
    coef, stiff, jac, fproj, nproj, lift, floc, fnei, clus, slots, orient, slist,
    out,
    wf, w_d, w_u, w_n, w_l, oh_loc, oh_rem, oh_send, or_rem,
    rhs, sp, own, upd, app, pend, wt, trn, tn, tl_hi, tl_lo, flux, rhs_l, rhs_r, tt,
    send, recv, send_sem, recv_sem,
):
    sub, dom = lax.axis_index("sub"), lax.axis_index("dom")
    subs, doms = lax.axis_size("sub"), lax.axis_size("dom")
    peers = ({"sub": sub - 1}, {"sub": sub + 1}, {"dom": dom - 1}, {"dom": dom + 1})
    has = (sub > 0, sub < subs - 1, dom > 0, dom < doms - 1)
    barrier = pltpu.get_barrier_semaphore()
    for r in range(4):
        @pl.when(has[r])
        def _():
            pl.semaphore_signal(barrier, inc=1, device_id=peers[r], device_id_type=MESH)

        @pl.when(jnp.logical_not(has[r]))
        def _():
            for j in range(SUBSTEPS):
                recv[j, r] = jnp.zeros((R, 512), F32)

    def copy(j, r, slot):
        return pltpu.make_async_remote_copy(
            src_ref=send.at[j, r],
            dst_ref=recv.at[j, slot],
            send_sem=send_sem.at[j, r],
            recv_sem=recv_sem.at[j, slot],
            device_id=peers[r],
            device_id_type=MESH,
        )

    def spots(rows, width, step, low):
        column, row = iota((rows, width), 1), iota((rows, width), 0)
        part = (column >= 2 * step) & (column < 3 * step) if low else column < 2 * step
        return onehot((column % step == row) & part)

    def triple(x, at):
        hi, lo = halves(x)
        return mm(hi, at[0]) + mm(lo, at[1])

    def turned(x, at, eye):
        hi, lo = halves(x)
        hi = lax.dot_general(eye, hi, NT, preferred_element_type=F32).astype(BF16)
        lo = lax.dot_general(eye, lo, NT, preferred_element_type=F32).astype(BF16)
        return mm(hi, at[0]) + mm(lo, at[1])

    wide = (spots(B, 192, 64, False), spots(B, 192, 64, True))
    for d in range(3):
        wf[d * B:(d + 1) * B, :] = triple(stiff[d], wide)
    w_d[...] = wf[0:3 * B, :].astype(BF16)

    def prepare_send():
        rows = iota((64, R), 0)
        picked = slist[0:1, :]
        picked = jnp.where(rows // R == 0, slist[0:1, :], jnp.where(
            rows // R == 1, slist[1:2, :], jnp.where(
                rows // R == 2, slist[2:3, :], slist[3:4, :])))
        picked = jnp.where(rows % R == iota((64, R), 1), picked.astype(F32), 0.0)
        column = jnp.sum(picked, axis=1, keepdims=True)
        oh_send[...] = onehot(iota((64, E), 1).astype(F32) == column)

    def prepare_rest():
        eye = onehot(iota((B, B), 0) == iota((B, B), 1))
        wide = (spots(B, 192, 64, False), spots(B, 192, 64, True))
        for d in range(3):
            wf[d * B:(d + 1) * B, :] = turned(stiff[d], wide, eye)
        zero = jnp.zeros((CP - C, 192), F32)
        for f in range(4):
            wf[3 * B + f * CP:3 * B + (f + 1) * CP, :] = jnp.concatenate(
                [triple(fproj[:, f, :], wide), zero], axis=0)
        w_u[...] = wf[0:3 * B + 4 * CP, :].astype(BF16)
        for o in range(ORIENTS):
            wf[o * CP:(o + 1) * CP, :] = jnp.concatenate([triple(nproj[o], wide), zero], axis=0)
        w_n[...] = wf[...].astype(BF16)
        total = None
        for f in range(4):
            column, row = iota((C, 288), 1), iota((C, 288), 0) + f * CP
            at = (onehot((column % 96 == row) & (column < 192)), onehot((column % 96 == row) & (column >= 192)))
            part = turned(lift[:, f, :], at, eye)
            total = part if total is None else total + part
        w_l[...] = total.astype(BF16)
        for f in range(4):
            cols = slice(f * E, (f + 1) * E)
            row = jnp.broadcast_to(slots[f:f + 1, :], (E, E))
            pair = jnp.broadcast_to(orient[f:f + 1, :], (E, E))
            here = onehot(iota((E, E), 0) == row)
            for o in range(ORIENTS):
                oh_loc[o * E:(o + 1) * E, cols] = here * onehot(pair == o)
            entry = iota((E, E), 0)
            first = onehot(entry + E == row) * onehot(entry < 64)
            second = onehot(entry + 64 == row) * onehot(entry >= 64)
            for k in range(2):
                oh_rem[k * E:(k + 1) * E, f * E:(f + 1) * E] = first
                oh_rem[k * E:(k + 1) * E, 512 + f * E:512 + (f + 1) * E] = second
        total = None
        for f in range(4):
            row = jnp.broadcast_to(orient[f:f + 1, :].astype(F32), (8, E)).astype(BF16)
            both = oh_rem[0:E, f * E:(f + 1) * E] + oh_rem[0:E, 512 + f * E:512 + (f + 1) * E]
            part = lax.dot_general(row, both, NT, preferred_element_type=F32)
            total = part if total is None else total + part
        or_rem[...] = total

    prepare_send()
    app[...] = jnp.zeros((Q, B, E), F32)
    pend[...] = jnp.zeros((Q, B, E), F32)

    def split_store(x, q):
        hi, lo = halves(jnp.concatenate([x, jnp.zeros((64 - B, E), F32)], axis=0))
        cols = pl.ds(q * E if isinstance(q, int) else pl.multiple_of(q * E, E), E)
        rhs[0:64, cols] = hi
        rhs[64:128, cols] = lo
        rhs[128:192, cols] = hi

    def mix(g):
        acc = None
        for q in range(Q):
            for d in range(3):
                term = jac[pl.ds(3 * g, 3), q, d:d + 1, :] * sp[d * B:(d + 1) * B, q * E:(q + 1) * E][None]
                acc = term if acc is None else acc + term
        return acc

    def face_mix(g, f, flow, trace, acc=None):
        for q in range(Q):
            term = flow[pl.ds(3 * g, 3), q, f:f + 1, :] * trace(q)[None]
            acc = term if acc is None else acc + term
        return acc

    def substep(j, carry):
        c = clus[0:1, :]
        length = jnp.where(c == 0, 1, jnp.where(c == 1, 2, 4)).astype(jnp.int32)
        lower = (jnp.bitwise_and(j, length - 1)).astype(F32) * STEP_LENGTH
        upper = lower + STEP_LENGTH
        low_power, up_power = lower, upper
        for k in range(ORDER):
            wt[k:k + 1, :] = (up_power - low_power) * ((-1.0) ** k / math.factorial(k + 1))
            low_power, up_power = low_power * lower, up_power * upper
        for q in range(Q):
            current = coef[q] + app[q]
            own[q] = current * wt[0:1, :]
            split_store(current, q)

        def degree(k, carry):
            sp[0:3 * B, :] = mm(w_d[...], rhs[...])
            weight = wt[pl.ds(k, 1), :]

            def group(g, carry):
                acc = mix(g)
                own[pl.ds(3 * g, 3)] = own[pl.ds(3 * g, 3)] + acc * weight[None]
                for i in range(3):
                    split_store(acc[i], 3 * g + i)
                return carry

            lax.fori_loop(0, 3, group, 0, unroll=True)
            return carry

        lax.fori_loop(1, ORDER, degree, 0)

        flat = jnp.concatenate([own[...].reshape(Q * B, E), jnp.zeros((8, E), F32)], axis=0)
        hi, lo = halves(flat)
        picked = lax.dot_general(oh_send[...], hi, NT, preferred_element_type=F32)
        picked = picked + lax.dot_general(oh_send[...], lo, NT, preferred_element_type=F32)
        for r in range(4):
            send[j, r] = picked[r * R:(r + 1) * R, :]

        @pl.when(j == 0)
        def _():
            pl.semaphore_wait(barrier, sum(jnp.where(h, 1, 0) for h in has))

        for r in (3, 2, 1, 0):
            @pl.when(has[r])
            def _():
                copy(j, r, OPPOSITE[r]).start()

        @pl.when(j == 0)
        def _():
            prepare_rest()

        for q in range(Q):
            split_store(own[q], q)
        sp[...] = mm(w_u[...], rhs[...])

        def local(g, carry):
            upd[pl.ds(3 * g, 3)] = mix(g)
            return carry

        lax.fori_loop(0, 3, local, 0, unroll=True)
        tn[...] = mm(w_n[...], rhs[...])

        def turn(o, carry):
            rows = pl.ds(pl.multiple_of(o * CP, CP), CP)
            cols = pl.ds(pl.multiple_of(o * E, E), E)
            hi, lo = halves(jnp.concatenate([tn[rows, q * E:(q + 1) * E] for q in range(Q)], axis=0))
            tl_hi[:, cols] = hi
            tl_lo[:, cols] = lo
            return carry

        lax.fori_loop(0, ORIENTS, turn, 0)

        def near(n, carry):
            cols = pl.ds(pl.multiple_of(n * 256, 256), 256)
            trn[:, cols] = mm(tl_hi[...], oh_loc[:, cols]) + mm(tl_lo[...], oh_loc[:, cols])
            for i in range(2):
                f = 2 * n + i
                rows = pl.ds(pl.multiple_of(3 * B + f * CP, 8), CP)
                acc = None
                for q in range(Q):
                    term = floc[:, q, pl.ds(f, 1), :] * sp[rows, q * E:(q + 1) * E][None]
                    acc = term if acc is None else acc + term
                flux[:, pl.ds(pl.multiple_of(f * CP, 8), CP), :] = acc
            return carry

        lax.fori_loop(0, 2, near, 0, unroll=True)

        for r in range(4):
            @pl.when(has[r])
            def _():
                copy(j, r, r).wait_recv()

        got = recv[j].reshape(64, 512)
        tt[...] = jnp.concatenate([got, got], axis=0).T
        left = iota((B, E), 1) < 64
        for i in range(5):
            first = tt[2 * i * B:(2 * i + 1) * B, :]
            second = tt[(2 * i + 1) * B:(2 * i + 2) * B, :] if i < 4 else first
            x = jnp.where(left, first, second)
            hi, lo = halves(jnp.concatenate([x, jnp.zeros((64 - B, E), F32)], axis=0))
            cols = slice(i * E, (i + 1) * E)
            rhs_r[0:64, cols] = hi
            rhs_r[64:128, cols] = lo
            rhs_r[128:192, cols] = hi
        traces = mm(w_n[...], rhs_r[...])
        pair = jnp.broadcast_to(or_rem[0:1, :], (CP, E))
        parts = []
        for i in range(5):
            cols = slice(i * E, (i + 1) * E)
            chosen = traces[0:CP, cols]
            for o in range(1, ORIENTS):
                chosen = jnp.where(pair == float(o), traces[o * CP:(o + 1) * CP, cols], chosen)
            parts.append(chosen)
        hi, lo = halves(jnp.concatenate(parts, axis=0))
        far = mm(jnp.concatenate([hi, lo], axis=1), oh_rem[...])
        for q in range(Q):
            rows = slice(q * CP, (q + 1) * CP)
            trn[rows, :] = trn[rows, :] + far[
                (q // 2) * CP:(q // 2 + 1) * CP, (q % 2) * 512:(q % 2) * 512 + 512]

        def outer(g, carry):
            parts = []
            for f in range(4):
                parts.append(face_mix(
                    g, f, fnei, lambda q: trn[q * CP:(q + 1) * CP, f * E:(f + 1) * E],
                    flux[pl.ds(3 * g, 3), f * CP:(f + 1) * CP, :]))
            for i in range(3):
                hi, lo = halves(jnp.concatenate([part[i] for part in parts], axis=0))
                cols = pl.ds(pl.multiple_of((3 * g + i) * E, E), E)
                rhs_l[0:96, cols] = hi
                rhs_l[96:192, cols] = lo
                rhs_l[192:288, cols] = hi
            return carry

        lax.fori_loop(0, 3, outer, 0, unroll=True)
        lifted = mm(w_l[...], rhs_l[...])
        finished = jnp.broadcast_to(jnp.where(jnp.bitwise_and(j + 1, length - 1) == 0, 1.0, 0.0), (B, E)) > 0.5
        for p in range(Q):
            total = pend[p] + (upd[p] - lifted[:, p * E:(p + 1) * E])
            app[p] = app[p] + jnp.where(finished, total, 0.0)
            pend[p] = jnp.where(finished, 0.0, total)
        return carry

    lax.fori_loop(0, SUBSTEPS, substep, 0)
    out[...] = app[...]

    def drain(j, carry):
        for r in range(4):
            @pl.when(has[r])
            def _():
                copy(j, r, OPPOSITE[r]).wait_send()
        return carry

    lax.fori_loop(0, SUBSTEPS, drain, 0)


def on_device(coefficients, stiffness, jacobians, face_proj, neigh_proj, lifting, flux_local,
              flux_neigh, clusters, face_slots, orientation, send_list):
    vmem = pl.BlockSpec(memory_space=pltpu.VMEM)
    return pl.pallas_call(
        kernel,
        out_shape=jax.ShapeDtypeStruct((Q, B, E), F32),
        in_specs=[vmem] * 12,
        out_specs=vmem,
        scratch_shapes=[
            pltpu.VMEM((288, 192), F32),
            pltpu.VMEM((168, 192), BF16),
            pltpu.VMEM((264, 192), BF16),
            pltpu.VMEM((288, 192), BF16),
            pltpu.VMEM((B, 288), BF16),
            pltpu.VMEM((ORIENTS * E, 512), BF16),
            pltpu.VMEM((256, 1024), BF16),
            pltpu.VMEM((64, E), BF16),
            pltpu.VMEM((8, E), F32),
            pltpu.VMEM((192, Q * E), BF16),
            pltpu.VMEM((264, Q * E), F32),
            pltpu.VMEM((Q, B, E), F32),
            pltpu.VMEM((Q, B, E), F32),
            pltpu.VMEM((Q, B, E), F32),
            pltpu.VMEM((Q, B, E), F32),
            pltpu.VMEM((8, E), F32),
            pltpu.VMEM((Q * CP, 512), F32),
            pltpu.VMEM((288, Q * E), F32),
            pltpu.VMEM((Q * CP, ORIENTS * E), BF16),
            pltpu.VMEM((Q * CP, ORIENTS * E), BF16),
            pltpu.VMEM((Q, 96, E), F32),
            pltpu.VMEM((288, Q * E), BF16),
            pltpu.VMEM((192, 640), BF16),
            pltpu.VMEM((512, E), F32),
            pltpu.VMEM((SUBSTEPS, 4, R, 512), F32),
            pltpu.VMEM((SUBSTEPS, 4, R, 512), F32),
            pltpu.SemaphoreType.DMA((SUBSTEPS, 4)),
            pltpu.SemaphoreType.DMA((SUBSTEPS, 4)),
        ],
        compiler_params=pltpu.CompilerParams(collective_id=0, has_side_effects=True),
    )(coefficients, stiffness, jacobians.transpose(1, 2, 0, 3), face_proj.transpose(1, 0, 2), neigh_proj,
      lifting.transpose(2, 0, 1), flux_local.transpose(1, 2, 0, 3), flux_neigh.transpose(1, 2, 0, 3),
      clusters.reshape(1, E), face_slots, orientation, send_list)


def solution(mesh):
    placed = (
        P(None, None, ("dom", "sub")),
        P(),
        P(None, None, None, ("dom", "sub")),
        P(),
        P(),
        P(),
        P(None, None, None, ("dom", "sub")),
        P(None, None, None, ("dom", "sub")),
        P(("dom", "sub")),
        P(None, ("dom", "sub")),
        P(None, ("dom", "sub")),
        P(None, ("dom", "sub")),
    )
    return jax.shard_map(
        on_device,
        mesh=mesh,
        in_specs=placed,
        out_specs=P(None, None, ("dom", "sub")),
        check_vma=False,
    )
```
